32 devices in a mesh: member: 8 (over z, y), grid: 4 (over x, core).
Axes of the slice: x: 2, y: 2, z: 4, core: 2. Of those that a mesh axis runs over, the one named last changes fastest.
Arguments:
- latents: bfloat16 [16, 4096, 1024], P('member', 'grid'), may hold values from -6 to 6
- w_in: bfloat16 [1024, 1024], replicated, may hold values from -0.1875 to 0.1875
- b_in: float32 [1024], replicated, may hold values from -3 to 3
- w_out: bfloat16 [1024, 96], replicated, may hold values from -0.1875 to 0.1875
- b_out: float32 [96], replicated, may hold values from -3 to 3
- target: float32 [96, 4096], P('member', 'grid'), may hold values from -6 to 6
- area_weight: float32 [4096], P('grid'), may hold values from 0.25 to 10
- var_weight: float32 [96], P('member'), may hold values from 0.25 to 10
- smoothers: float32 [2, 32, 4, 128, 128], P(None, 'grid'), may hold values from -0.25 to 0.25
- block_index: int32 [2, 32, 4], P(None, 'grid'), may hold values from 0 to 31, as said below
- block_count: int32 [2, 32], P(None, 'grid'), may hold values from 1 to 4, as said below
Outputs:
- grad_latent: bfloat16 [16, 4096, 1024], P('member', 'grid')
- loss: float32 [], replicated
The draws below stay inside these ranges and needn't reach their ends.
Inputs may be any that keep to these rules, and one draw needn't show every extreme that they name: `block_index`: block row r lists blocks that lie at most 8 blocks from r on either side; that distance is reached on both sides in some rows; entries of a row may repeat. Only the first block_count[s, r] slots of block row r are used.
All inputs are finite; a program needn't handle non-finite values.
Results may differ from the reference program's by a relative error of at most 0.008.
Values may be sent and summed in bfloat16 or wider, within the bound.
No kernel may reach another device: no remote copies, remote signals or barrier semaphores. Data moves between devices by JAX's collectives and lax.ppermute only.
A program may use at most 64 MiB of HBM per device.

```python
import functools
import math
import jax
import jax.numpy as jnp
from jax import lax

LATENT = 1024
FFN_WIDTH = 1024
VARS = 96
MEMBERS = 16
SCALES = 2
BLOCK = 128
KMAX = 4
PTS_DEV = 1024
NPTS = 4096
NBLK = 32


def draw_block_index(key, part):
    key = jax.random.fold_in(key, 11)
    reach = PTS_DEV // BLOCK
    rows = jnp.arange(NBLK, dtype=jnp.int32)
    lowest = jnp.maximum(rows - reach, 0)[None, :, None]
    upmost = jnp.minimum(rows + reach, NBLK - 1)[None, :, None]
    offset = jax.random.randint(key, (SCALES, NBLK, KMAX), 0, 2 * reach + 1, dtype=jnp.int32)
    picked = jnp.clip(rows[None, :, None] - reach + offset, lowest, upmost)
    slot = jnp.arange(KMAX, dtype=jnp.int32)[None, None, :]
    forced = (rows % 3 == 1)[None, :, None]
    picked = jnp.where(forced & (slot == 0), lowest, picked)
    picked = jnp.where(forced & (slot == 1), upmost, picked)
    return picked.astype(jnp.int32)


def draw_block_count(key, part):
    key = jax.random.fold_in(key, 23)
    rows = jnp.arange(NBLK, dtype=jnp.int32)
    counts = jax.random.randint(key, (SCALES, NBLK), 1, KMAX + 1, dtype=jnp.int32)
    counts = jnp.where((rows % 3 == 1)[None, :], KMAX, counts)
    return counts.astype(jnp.int32)


def draw_area_weight(key, part):
    key = jax.random.fold_in(key, 31)
    place = jnp.arange(NPTS, dtype=jnp.float32) / max(NPTS - 1, 1)
    noise = jnp.exp(jax.random.uniform(key, (NPTS,), jnp.float32, math.log(0.3), math.log(3.0)))
    ramp = 1.0 + 2.0 * place
    return (noise * ramp).astype(jnp.float32)


def draw_var_weight(key, part):
    key = jax.random.fold_in(key, 37)
    place = jnp.arange(VARS, dtype=jnp.float32) / max(VARS - 1, 1)
    noise = jnp.exp(jax.random.uniform(key, (VARS,), jnp.float32, math.log(0.3), math.log(3.0)))
    ramp = 1.0 + 2.0 * place
    return (noise * ramp).astype(jnp.float32)


def block_levels(own_key, dims, cuts, low, largest):
    level = 1.0
    for axis_at, parts in cuts:
        steps = jax.random.uniform(jax.random.fold_in(jax.random.fold_in(own_key, 6), axis_at), (parts,), jnp.float32, low / len(cuts), largest / len(cuts))
        level = level * jnp.repeat(jnp.exp(steps), dims[axis_at] // parts).reshape((-1,) + (1,) * (len(dims) - 1 - axis_at))
    return level


def bell_draw(rng, extent, scale, bound, shards=(), kind=jnp.bfloat16):
    values = jax.random.normal(rng, extent, jnp.float32) * scale
    if len(shards) > 0:
        values = block_levels(rng, extent, shards, -0.22, 0.18) * values
    return jnp.clip(values, min=-bound, max=bound).astype(kind)


def setup_inputs(seed: int = 0) -> dict:
    streams_of = jax.random.split(jax.random.key(seed), 12)
    return {
        "latents": bell_draw(streams_of[0], (MEMBERS, NPTS, LATENT), 1.0, 6.0, ((0, 8), (1, 4))),
        "w_in": bell_draw(streams_of[1], (LATENT, FFN_WIDTH), LATENT ** -0.5, 0.1875),
        "b_in": bell_draw(streams_of[2], (FFN_WIDTH,), 0.5, 3.0, (), jnp.float32),
        "w_out": bell_draw(streams_of[3], (FFN_WIDTH, VARS), FFN_WIDTH ** -0.5, 0.1875),
        "b_out": bell_draw(streams_of[4], (VARS,), 0.5, 3.0, (), jnp.float32),
        "target": bell_draw(streams_of[5], (VARS, NPTS), 1.0, 6.0, ((0, 8), (1, 4)), jnp.float32),
        "area_weight": draw_area_weight(jax.random.fold_in(streams_of[11], 71), 0),
        "var_weight": draw_var_weight(jax.random.fold_in(streams_of[11], 71), 0),
        "smoothers": bell_draw(streams_of[8], (SCALES, NBLK, KMAX, BLOCK, BLOCK), (KMAX * BLOCK) ** -0.5, 0.25, ((1, 4),), jnp.float32),
        "block_index": draw_block_index(jax.random.fold_in(streams_of[11], 71), 0),
        "block_count": draw_block_count(jax.random.fold_in(streams_of[11], 71), 0),
    }


kernel_eps = 0.01
highest = lax.Precision.HIGHEST

def wide_dot(left, right):
    return jnp.dot(left.astype(jnp.float32), right.astype(jnp.float32), precision=highest, preferred_element_type=jnp.float32)

def mask_weights(smoother, counts):
    live = (jnp.arange(KMAX, dtype=jnp.int32)[None, :] < counts[:, None]).astype(jnp.float32)
    return smoother * live[:, :, None, None]

def smooth_global(field_rows, masked, indices):
    height = field_rows.shape[0]
    blocks = field_rows.reshape(height, NBLK, BLOCK)
    picked = jnp.take(blocks, indices, axis=1)
    result = jnp.einsum('rbkp,bkpq->rbq', picked, masked, precision=highest)
    return result.reshape(height, NPTS)

def adjoint_global(grad_rows, masked, indices):
    height = grad_rows.shape[0]
    blocks = grad_rows.reshape(height, NBLK, BLOCK)
    contrib = jnp.einsum('rbq,bkpq->rbkp', blocks, masked, precision=highest)
    onehot = (indices[:, :, None] == jnp.arange(NBLK, dtype=jnp.int32)[None, None, :]).astype(jnp.float32)
    result = jnp.einsum('rbkp,bkc->rcp', contrib, onehot, precision=highest)
    return result.reshape(height, NPTS)

def ensemble_loss(fields, truth, weight_grid):
    members = fields.shape[0]
    spread = fields[:, None] - fields[None, :]
    kernel = jnp.sqrt(spread * spread + kernel_eps)
    miss = fields - truth[None]
    kernel_miss = jnp.sqrt(miss * miss + kernel_eps)
    score = lax.optimization_barrier(jnp.mean(kernel_miss, 0)) - (lax.optimization_barrier(jnp.sum(kernel, (0, 1))) - members * math.sqrt(kernel_eps)) / (2.0 * members * (members - 1))
    total = jnp.sum(weight_grid * score)
    grad = weight_grid[None] * (miss / kernel_miss - lax.optimization_barrier(jnp.sum(spread / kernel, 1)) / (members - 1))
    return (total, grad)

def score_variable(packed):
    return ensemble_loss(packed[0], packed[1], packed[2])

def reference(latents, w_in, b_in, w_out, b_out, target, area_weight, var_weight, smoothers, block_index, block_count):

    def forward(latent_rows):
        pre_act = wide_dot(latent_rows, w_in) + b_in
        hidden = jax.nn.gelu(pre_act).astype(jnp.bfloat16)
        return wide_dot(hidden, w_out).T + b_out[:, None]
    predicted = lax.map(forward, latents)
    rounded = lax.optimization_barrier(predicted.astype(jnp.bfloat16)).astype(jnp.float32)
    truth_round = lax.optimization_barrier(target.astype(jnp.bfloat16)).astype(jnp.float32)
    layers = [predicted]
    truths = [target]
    masks = []
    for scale in range(SCALES):
        masked = mask_weights(smoothers[scale], block_count[scale])
        masks.append(masked)
        smoother_fn = functools.partial(smooth_global, masked=masked, indices=block_index[scale])
        layers.append(lax.map(smoother_fn, rounded))
        truths.append(smooth_global(truth_round, masked, block_index[scale]))
    weight_grid = var_weight[:, None] * area_weight[None, :]
    total = jnp.zeros((), jnp.float32)
    layer_grads = []
    for layer_field, layer_truth in zip(layers, truths):
        totals, grads = lax.map(score_variable, (jnp.swapaxes(layer_field, 0, 1), layer_truth, weight_grid))
        total = total + jnp.sum(totals)
        layer_grads.append(jnp.swapaxes(grads, 0, 1))
    field_grad = layer_grads[0]
    for scale in range(SCALES):
        adjoint_fn = functools.partial(adjoint_global, masked=masks[scale], indices=block_index[scale])
        field_grad = field_grad + lax.map(adjoint_fn, layer_grads[scale + 1])

    def backward(packed):
        latent_rows, grad_rows = packed
        pre_act = wide_dot(latent_rows, w_in) + b_in
        _, gelu_back = jax.vjp(jax.nn.gelu, pre_act)
        grad_round = lax.optimization_barrier(grad_rows.astype(jnp.bfloat16))
        hidden_grad = wide_dot(grad_round.T, w_out.T)
        pre_grad = lax.optimization_barrier(gelu_back(hidden_grad)[0].astype(jnp.bfloat16))
        return wide_dot(pre_grad, w_in.T).astype(jnp.bfloat16)
    grad_latent = lax.map(backward, (latents, field_grad))
    loss = total / ((SCALES + 1) * VARS * NPTS)
    return (grad_latent, loss)
```

```python
import functools
import math

import jax
import jax.numpy as jnp
import numpy as np
from jax import lax
from jax.experimental import pallas as pl
from jax.experimental.pallas import tpu as pltpu
from jax.sharding import PartitionSpec as P

kernel_eps = 0.01
f32 = jnp.float32
bf16 = jnp.bfloat16
SUB = 8
GELU_C = math.sqrt(2.0 / math.pi)
GELU_A = 0.044715
VMEM_LIMIT = 60 * 1024 * 1024


class Layout:
    def __init__(self, senders, own_members, variables, blocks, block):
        self.senders = senders
        self.own = own_members
        self.vars = variables
        self.blocks = blocks
        self.block = block
        rest = variables % SUB
        self.half = 0 < rest <= SUB // 2 and own_members % 2 == 0 and blocks % 2 == 0
        self.whole = variables // SUB if self.half or rest == 0 else variables // SUB + 1
        self.piece = own_members * (self.whole * SUB + (SUB // 2 if self.half else 0))
        self.rows = senders * self.piece
        self.members = senders * own_members
        self.tiles = blocks * self.whole + (blocks // 2 if self.half else 0)
        self.truth_rows = -(-variables // 16) * 16
        self.total_rows = self.rows + self.truth_rows

    def permutation(self):
        out = np.zeros((self.own, self.senders * self.vars, self.rows), np.float32)
        for sender in range(self.senders):
            for c in range(self.piece):
                if c < self.whole * self.own * SUB:
                    v = c // (self.own * SUB) * SUB + c % SUB
                    m = c // SUB % self.own
                else:
                    tail = c - self.whole * self.own * SUB
                    v = self.whole * SUB + tail % (SUB // 2)
                    m = tail // (SUB // 2)
                if v < self.vars:
                    out[m, sender * self.vars + v, sender * self.piece + c] = 1.0
        return out


def low_half():
    return lax.broadcasted_iota(jnp.int32, (SUB, 128), 0) < SUB // 2


def swap(x):
    return pltpu.roll(x, SUB // 2, 0)


def rows_to_tiles(lay, take, put, put_truth):
    step = 2 if lay.half else 1
    for r0 in range(0, lay.blocks, step):
        rows = [take(r0 + d) for d in range(step)]
        for d in range(step):
            for a in range(lay.whole):
                t = (r0 + d) * lay.whole + a
                for sender in range(lay.senders):
                    for m in range(lay.own):
                        at = sender * lay.piece + (a * lay.own + m) * SUB
                        put(t, sender * lay.own + m, rows[d][at : at + SUB])
                at = lay.rows + a * SUB
                put_truth(t, rows[d][at : at + SUB])
        if lay.half:
            t = lay.blocks * lay.whole + r0 // 2
            low = low_half()
            for sender in range(lay.senders):
                for m in range(0, lay.own, 2):
                    at = sender * lay.piece + lay.whole * lay.own * SUB + m * (SUB // 2)
                    first, second = rows[0][at : at + SUB], rows[1][at : at + SUB]
                    put(t, sender * lay.own + m, jnp.where(low, first, swap(second)))
                    put(t, sender * lay.own + m + 1, jnp.where(low, swap(first), second))
            at = lay.rows + lay.whole * SUB
            first, second = rows[0][at : at + SUB], rows[1][at : at + SUB]
            put_truth(t, jnp.where(low, first, swap(second)))


def tiles_to_rows(lay, get, put):
    for r in range(lay.blocks):
        for sender in range(lay.senders):
            for a in range(lay.whole):
                for m in range(lay.own):
                    at = sender * lay.piece + (a * lay.own + m) * SUB
                    put(r, at, get(r * lay.whole + a, sender * lay.own + m))
            if lay.half:
                t = lay.blocks * lay.whole + r // 2
                low = low_half()
                for m in range(0, lay.own, 2):
                    at = sender * lay.piece + lay.whole * lay.own * SUB + m * (SUB // 2)
                    first = get(t, sender * lay.own + m)
                    second = get(t, sender * lay.own + m + 1)
                    if r % 2 == 0:
                        put(r, at, jnp.where(low, first, swap(second)))
                    else:
                        put(r, at, jnp.where(low, swap(first), second))


def crps_tile(x, y, w):
    members = len(x)
    pair_total = None
    pulls = [None] * members
    for i in range(members):
        for j in range(i + 1, members):
            d = x[i] - x[j]
            t = d * d + kernel_eps
            inv = lax.rsqrt(t)
            k = t * inv
            dk = d * inv
            pair_total = k if pair_total is None else pair_total + k
            pulls[i] = dk if pulls[i] is None else pulls[i] + dk
            pulls[j] = -dk if pulls[j] is None else pulls[j] - dk
    miss_total = None
    grads = []
    for i in range(members):
        d = x[i] - y
        t = d * d + kernel_eps
        inv = lax.rsqrt(t)
        k = t * inv
        miss_total = k if miss_total is None else miss_total + k
        grads.append(w * (d * inv - pulls[i] * (1.0 / (members - 1))))
    score = miss_total * (1.0 / members) - pair_total * (1.0 / (members * (members - 1)))
    return w * score, grads


def crps_loop(lay, x_ref, y_ref, w_ref, total_ref):
    def step(t, total):
        x = [x_ref[t, m] for m in range(lay.members)]
        part, grads = crps_tile(x, y_ref[t], w_ref[t])
        for m in range(lay.members):
            x_ref[t, m] = grads[m]
        return total + part

    total_ref[...] = lax.fori_loop(0, lay.tiles, step, total_ref[...])


def fwd_kernel(lay, lat_ref, w_in_ref, b_in_ref, w_out_ref, perm_ref, b_out_ref, hi_ref, lo_ref, pre_ref, a_scr, bias_scr):
    @pl.when(pl.program_id(0) == 0)
    def _():
        spread = None
        for m in range(lay.own):
            p = perm_ref[m]
            a_scr[m] = jnp.dot(w_out_ref[...], p, preferred_element_type=f32).astype(bf16)
            spread = p.astype(f32) if spread is None else spread + p.astype(f32)
        bias = jnp.broadcast_to(b_out_ref[...], (SUB, b_out_ref.shape[1]))
        bias_scr[...] = jnp.dot(bias, spread, precision=lax.Precision.HIGHEST, preferred_element_type=f32)

    acc = bias_scr[0:1, :]
    for m in range(lay.own):
        pre = jnp.dot(lat_ref[m], w_in_ref[...], preferred_element_type=f32) + b_in_ref[...]
        pre_ref[m] = pre.astype(bf16)
        inner = pre * (GELU_C + (GELU_C * GELU_A) * (pre * pre))
        half = 0.5 * pre
        hidden = (half + half * jnp.tanh(inner)).astype(bf16)
        acc = acc + jnp.dot(hidden, a_scr[m], preferred_element_type=f32)
    field = acc.T
    for sender in range(lay.senders):
        for r in range(hi_ref.shape[1]):
            part = field[sender * lay.piece : (sender + 1) * lay.piece, r * lay.block : (r + 1) * lay.block]
            hi = part.astype(bf16)
            hi_ref[sender, r] = hi
            lo_ref[sender, r] = (part - hi.astype(f32)).astype(bf16)


def prep_kernel(lay, slots, count_ref, pre_ref, w_in_ref, w_out_ref, permt_ref, sm_ref, slope_ref, w_int_ref, at_ref, wb_ref):
    x = pre_ref[...].astype(f32)
    sq = x * x
    t = jnp.tanh(x * (GELU_C + (GELU_C * GELU_A) * sq))
    half = 0.5 * (1.0 + t)
    tail = (0.5 * x) * (1.0 - t * t) * (GELU_C + (3.0 * GELU_C * GELU_A) * sq)
    slope_ref[...] = (half + tail).astype(bf16)
    w_int_ref[...] = w_in_ref[...].T
    scales, rows = sm_ref.shape[0], sm_ref.shape[1]
    step = pl.program_id(0)
    for s in range(scales):
        for r in range(rows):
            for k in range(slots):
                live = (k < count_ref[s, step * rows + r]).astype(f32)
                wb_ref[s, r, k * lay.block : (k + 1) * lay.block, :] = (sm_ref[s, r, k] * live).astype(bf16)

    for m in range(lay.own):
        at_ref[m] = lax.dot_general(
            permt_ref[m], w_out_ref[...], (((1,), (1,)), ((), ())), preferred_element_type=f32
        ).astype(bf16)


def raw_kernel(lay, vw_ref, area_ref, hi_ref, lo_ref, target_ref, grad_ref, w_ref, total_ref, x_scr, y_scr):
    rows = lax.broadcasted_iota(jnp.int32, (lay.truth_rows, lay.block), 0)
    column = jnp.zeros((lay.truth_rows, lay.block), f32)
    for v in range(lay.vars):
        column = jnp.where(rows == v, vw_ref[v], column)

    def weights(r):
        return column * area_ref[:, r * lay.block : (r + 1) * lay.block]

    def take(r):
        field = hi_ref[:, r].astype(f32) + lo_ref[:, r].astype(f32)
        truth = target_ref[:, r * lay.block : (r + 1) * lay.block]
        return jnp.concatenate([field.reshape(lay.rows, lay.block), truth], 0)

    def put(t, m, tile):
        x_scr[t, m] = tile

    def put_truth(t, tile):
        y_scr[t] = tile

    def put_weight(t, tile):
        w_ref[t] = tile

    rows_to_tiles(lay, take, put, put_truth)
    for r in range(lay.blocks):
        w = weights(r)
        for a in range(lay.whole):
            w_ref[r * lay.whole + a] = w[a * SUB : (a + 1) * SUB]
        if lay.half and r % 2:
            low = low_half()
            at = lay.whole * SUB
            first, second = weights(r - 1)[at : at + SUB], w[at : at + SUB]
            w_ref[lay.blocks * lay.whole + r // 2] = jnp.where(low, first, swap(second))
    total_ref[...] = jnp.zeros_like(total_ref)
    crps_loop(lay, x_scr, y_scr, w_ref, total_ref)

    def put_rows(r, at, tile):
        grad_ref[r, at : at + SUB] = tile

    tiles_to_rows(lay, lambda t, m: x_scr[t, m], put_rows)


def scales_kernel(lay, slots, pos_ref, left_ref, own_ref, right_ref, tl_ref, to_ref, tr_ref, wb_ref, w_ref, base_ref, total_in_ref, center_ref, lower_ref, upper_ref, loss_ref, ext_scr, x_scr, y_scr, total_scr, row_scr, adj_scr):
    scales = wb_ref.shape[0]
    block = lay.block
    for at, (src, truth) in enumerate(((left_ref, tl_ref), (own_ref, to_ref), (right_ref, tr_ref))):
        for r in range(lay.blocks):
            field = src[:, r].astype(f32).reshape(lay.rows, block)
            ext_scr[at * lay.blocks + r, : lay.rows] = field.astype(bf16)
            ext_scr[at * lay.blocks + r, lay.rows :] = truth[:, r * block : (r + 1) * block]
    adj_scr[...] = jnp.zeros_like(adj_scr)
    total_scr[...] = total_in_ref[...]
    for s in range(scales):

        def take(r):
            gathered = jnp.concatenate([ext_scr[pos_ref[s, r, k]] for k in range(slots)], 1)
            return jnp.dot(gathered, wb_ref[s, r], preferred_element_type=f32)

        def put(t, m, tile):
            x_scr[t, m] = tile

        def put_truth(t, tile):
            y_scr[t] = tile

        rows_to_tiles(lay, take, put, put_truth)
        crps_loop(lay, x_scr, y_scr, w_ref, total_scr)

        def put_rows(r, at, tile):
            row_scr[r, at : at + SUB] = tile

        tiles_to_rows(lay, lambda t, m: x_scr[t, m], put_rows)
        for r in range(lay.blocks):
            back = lax.dot_general(
                row_scr[r].astype(bf16), wb_ref[s, r], (((1,), (1,)), ((), ())), preferred_element_type=f32
            )
            for k in range(slots):
                p = pos_ref[s, r, k]
                adj_scr[p] = adj_scr[p] + back[:, k * block : (k + 1) * block]
    n = lay.blocks
    lower_ref[...] = adj_scr[0:n].astype(bf16)
    center_ref[...] = adj_scr[n : 2 * n] + base_ref[...]
    upper_ref[...] = adj_scr[2 * n : 3 * n].astype(bf16)
    loss_ref[...] = jnp.broadcast_to(jnp.sum(total_scr[...]), loss_ref.shape)


def join_kernel(lay, center_ref, a_ref, b_ref, out_ref):
    for r in range(lay.blocks):
        rows = center_ref[r] + (a_ref[r].astype(f32) + b_ref[r].astype(f32))
        out_ref[:, r] = rows.reshape(lay.senders, lay.piece, lay.block).astype(bf16)


def bwd_kernel(lay, g_ref, at_ref, slope_ref, w_int_ref, out_ref):
    cols = []
    for r in range(g_ref.shape[1]):
        rows = g_ref[:, r].astype(f32).reshape(lay.rows, lay.block)
        cols.append(rows.T.astype(bf16))
    grads = jnp.concatenate(cols, 0)
    for m in range(lay.own):
        hidden_grad = jnp.dot(grads, at_ref[m], preferred_element_type=f32)
        pre_grad = (hidden_grad * slope_ref[m].astype(f32)).astype(bf16)
        out_ref[m] = jnp.dot(pre_grad, w_int_ref[...], preferred_element_type=f32).astype(bf16)


def params():
    return pltpu.CompilerParams(vmem_limit_bytes=VMEM_LIMIT)


def cost(flops, nbytes, trans=0):
    return pl.CostEstimate(flops=int(flops), bytes_accessed=int(nbytes), transcendentals=int(trans))


VM = pl.BlockSpec(memory_space=pltpu.VMEM)
SM = pl.BlockSpec(memory_space=pltpu.SMEM)


def whole_spec(shape):
    return pl.BlockSpec(shape, lambda i: (0,) * len(shape))


def on_device(
    latents,
    w_in,
    b_in,
    w_out,
    b_out,
    target,
    area_weight,
    var_weight,
    smoothers,
    block_index,
    block_count,
):
    own, points, width = latents.shape
    hidden_width = w_in.shape[1]
    var_total = w_out.shape[1]
    var_local = target.shape[0]
    scales, blocks, slots, block, _ = smoothers.shape
    senders = lax.axis_size("member")
    devices_grid = lax.axis_size("grid")
    lay = Layout(senders, own, var_local, blocks, block)
    perm_np = lay.permutation()
    perm = jnp.asarray(perm_np, bf16)
    perm_t = jnp.asarray(perm_np.transpose(0, 2, 1), bf16)
    payload = (senders, blocks, lay.piece, block)

    tile = min(points, 256)
    steps = points // tile
    tile_blocks = tile // block
    payload_spec = pl.BlockSpec((senders, tile_blocks, lay.piece, block), lambda i: (0, i, 0, 0))
    wide_spec = pl.BlockSpec((own, tile, hidden_width), lambda i: (0, i, 0))
    hi, lo, pre = pl.pallas_call(
        functools.partial(fwd_kernel, lay),
        grid=(steps,),
        in_specs=[
            pl.BlockSpec((own, tile, width), lambda i: (0, i, 0)),
            whole_spec(w_in.shape),
            whole_spec((1, hidden_width)),
            whole_spec(w_out.shape),
            whole_spec(perm.shape),
            whole_spec((1, var_total)),
        ],
        out_specs=[payload_spec, payload_spec, wide_spec],
        out_shape=[
            jax.ShapeDtypeStruct(payload, bf16),
            jax.ShapeDtypeStruct(payload, bf16),
            jax.ShapeDtypeStruct((own, points, hidden_width), bf16),
        ],
        scratch_shapes=[pltpu.VMEM((own, hidden_width, lay.rows), bf16), pltpu.VMEM((SUB, lay.rows), f32)],
        compiler_params=params(),
        cost_estimate=cost(2 * own * points * width * hidden_width, 12e6, own * points * hidden_width),
        name="fwd",
    )(latents, w_in, b_in.reshape(1, -1), w_out, perm, b_out.reshape(1, -1))

    own_hi = lax.all_to_all(hi, "member", split_axis=0, concat_axis=0, tiled=True)
    own_lo = lax.all_to_all(lo, "member", split_axis=0, concat_axis=0, tiled=True)

    prep_steps = math.gcd(blocks, 4)
    prep_rows = blocks // prep_steps
    prep_tile = points // prep_steps
    prep_cols = hidden_width // prep_steps
    slope, w_in_t, a_t, wb = pl.pallas_call(
        functools.partial(prep_kernel, lay, slots),
        grid=(prep_steps,),
        in_specs=[
            SM,
            pl.BlockSpec((own, prep_tile, hidden_width), lambda i: (0, i, 0)),
            pl.BlockSpec((width, prep_cols), lambda i: (0, i)),
            pl.BlockSpec((prep_cols, var_total), lambda i: (i, 0)),
            whole_spec(perm_t.shape),
            pl.BlockSpec((scales, prep_rows, slots, block, block), lambda i: (0, i, 0, 0, 0)),
        ],
        out_specs=[
            pl.BlockSpec((own, prep_tile, hidden_width), lambda i: (0, i, 0)),
            pl.BlockSpec((prep_cols, width), lambda i: (i, 0)),
            pl.BlockSpec((own, lay.rows, prep_cols), lambda i: (0, 0, i)),
            pl.BlockSpec((scales, prep_rows, slots * block, block), lambda i: (0, i, 0, 0)),
        ],
        out_shape=[
            jax.ShapeDtypeStruct((own, points, hidden_width), bf16),
            jax.ShapeDtypeStruct((hidden_width, width), bf16),
            jax.ShapeDtypeStruct((own, lay.rows, hidden_width), bf16),
            jax.ShapeDtypeStruct((scales, blocks, slots * block, block), bf16),
        ],
        compiler_params=params(),
        cost_estimate=cost(2e9, 2e7, own * points * hidden_width),
        name="prep",
    )(block_count, pre, w_in, w_out, perm_t, smoothers)

    _, target = lax.optimization_barrier((pre, target))
    target_pad = jnp.pad(target, ((0, lay.truth_rows - var_local), (0, 0)))
    truth = target_pad.astype(bf16)
    up = [(i, i + 1) for i in range(devices_grid - 1)]
    down = [(i + 1, i) for i in range(devices_grid - 1)]
    truth_left = lax.ppermute(truth, "grid", up)
    truth_right = lax.ppermute(truth, "grid", down)
    field_left = lax.ppermute(own_hi, "grid", up)
    field_right = lax.ppermute(own_hi, "grid", down)

    grad_shape = (blocks, lay.rows, block)
    tile_shape = (lay.tiles, lay.members, SUB, block)
    base, w_tiles, total = pl.pallas_call(
        functools.partial(raw_kernel, lay),
        in_specs=[SM, VM, VM, VM, VM],
        out_specs=[VM, VM, VM],
        out_shape=[
            jax.ShapeDtypeStruct(grad_shape, f32),
            jax.ShapeDtypeStruct((lay.tiles, SUB, block), f32),
            jax.ShapeDtypeStruct((SUB, block), f32),
        ],
        scratch_shapes=[pltpu.VMEM(tile_shape, f32), pltpu.VMEM((lay.tiles, SUB, block), f32)],
        compiler_params=params(),
        cost_estimate=cost(5e8, 3e6, 2e6),
        name="raw",
    )(var_weight, area_weight.reshape(1, -1), own_hi, own_lo, target_pad)

    positions = jnp.clip(block_index - (lax.axis_index("grid") - 1) * blocks, 0, 3 * blocks - 1)
    device_count = senders * devices_grid
    center, lower, upper, losses = pl.pallas_call(
        functools.partial(scales_kernel, lay, slots),
        in_specs=[SM] + [VM] * 10,
        out_specs=[VM] * 4,
        out_shape=[
            jax.ShapeDtypeStruct(grad_shape, f32),
            jax.ShapeDtypeStruct(grad_shape, bf16),
            jax.ShapeDtypeStruct(grad_shape, bf16),
            jax.ShapeDtypeStruct((device_count, block), f32),
        ],
        scratch_shapes=[
            pltpu.VMEM((3 * blocks, lay.total_rows, block), bf16),
            pltpu.VMEM(tile_shape, f32),
            pltpu.VMEM((lay.tiles, SUB, block), f32),
            pltpu.VMEM((SUB, block), f32),
            pltpu.VMEM(grad_shape, f32),
            pltpu.VMEM((3 * blocks, lay.rows, block), f32),
        ],
        compiler_params=params(),
        cost_estimate=cost(2e9, 8e6, 4e6),
        name="scales",
    )(positions, field_left, own_hi, field_right, truth_left, truth, truth_right, wb, w_tiles, base, total)

    from_upper = lax.ppermute(lower, "grid", down)
    from_lower = lax.ppermute(upper, "grid", up)
    joined = pl.pallas_call(
        functools.partial(join_kernel, lay),
        in_specs=[VM] * 3,
        out_specs=VM,
        out_shape=jax.ShapeDtypeStruct(payload, bf16),
        compiler_params=params(),
        cost_estimate=cost(1e6, 2e6),
        name="join",
    )(center, from_upper, from_lower)
    field_grad = lax.all_to_all(joined, "member", split_axis=0, concat_axis=0, tiled=True)
    parts = lax.all_to_all(losses, ("member", "grid"), split_axis=0, concat_axis=0, tiled=True)
    loss = jnp.sum(parts[:, 0]) / ((scales + 1) * var_total * points * devices_grid)

    grad = pl.pallas_call(
        functools.partial(bwd_kernel, lay),
        grid=(steps,),
        in_specs=[
            payload_spec,
            whole_spec(a_t.shape),
            wide_spec,
            whole_spec(w_in_t.shape),
        ],
        out_specs=pl.BlockSpec((own, tile, width), lambda i: (0, i, 0)),
        out_shape=jax.ShapeDtypeStruct((own, points, width), bf16),
        compiler_params=params(),
        cost_estimate=cost(2 * own * points * width * hidden_width, 12e6),
        name="bwd",
    )(field_grad, a_t, slope, w_in_t)
    return grad, loss


def solution(mesh):
    in_specs = (
        P("member", "grid", None),
        P(),
        P(),
        P(),
        P(),
        P("member", "grid"),
        P("grid"),
        P("member"),
        P(None, "grid", None, None, None),
        P(None, "grid", None),
        P(None, "grid"),
    )
    out_specs = (P("member", "grid", None), P())
    return jax.shard_map(
        on_device, mesh=mesh, in_specs=in_specs, out_specs=out_specs, check_vma=False
    )
```

```python
import functools
import math

import jax
import jax.numpy as jnp
import numpy as np
from jax import lax
from jax.experimental import pallas as pl
from jax.experimental.pallas import tpu as pltpu
from jax.sharding import PartitionSpec as P

kernel_eps = 0.01
f32 = jnp.float32
bf16 = jnp.bfloat16
SUB = 8
GELU_C = math.sqrt(2.0 / math.pi)
GELU_A = 0.044715


class Layout:
    def __init__(self, senders, own_members, variables, blocks, block):
        self.senders = senders
        self.own = own_members
        self.vars = variables
        self.blocks = blocks
        self.block = block
        rest = variables % SUB
        self.half = 0 < rest <= SUB // 2 and own_members % 2 == 0 and blocks % 2 == 0
        self.whole = variables // SUB if self.half or rest == 0 else variables // SUB + 1
        self.piece = own_members * (self.whole * SUB + (SUB // 2 if self.half else 0))
        self.rows = senders * self.piece
        self.members = senders * own_members
        self.tiles = blocks * self.whole + (blocks // 2 if self.half else 0)
        self.truth_rows = -(-variables // 16) * 16
        self.total_rows = self.rows + self.truth_rows

    def permutation(self):
        out = np.zeros((self.own, self.senders * self.vars, self.rows), np.float32)
        for sender in range(self.senders):
            for c in range(self.piece):
                if c < self.whole * self.own * SUB:
                    v = c // (self.own * SUB) * SUB + c % SUB
                    m = c // SUB % self.own
                else:
                    tail = c - self.whole * self.own * SUB
                    v = self.whole * SUB + tail % (SUB // 2)
                    m = tail // (SUB // 2)
                if v < self.vars:
                    out[m, sender * self.vars + v, sender * self.piece + c] = 1.0
        return out


def low_half():
    return lax.broadcasted_iota(jnp.int32, (SUB, 128), 0) < SUB // 2


def swap(x):
    return pltpu.roll(x, SUB // 2, 0)


def rows_to_tiles(lay, take, put, put_truth):
    step = 2 if lay.half else 1
    for r0 in range(0, lay.blocks, step):
        rows = [take(r0 + d) for d in range(step)]
        for d in range(step):
            for a in range(lay.whole):
                t = (r0 + d) * lay.whole + a
                for sender in range(lay.senders):
                    for m in range(lay.own):
                        at = sender * lay.piece + (a * lay.own + m) * SUB
                        put(t, sender * lay.own + m, rows[d][at : at + SUB])
                at = lay.rows + a * SUB
                put_truth(t, rows[d][at : at + SUB])
        if lay.half:
            t = lay.blocks * lay.whole + r0 // 2
            low = low_half()
            for sender in range(lay.senders):
                for m in range(0, lay.own, 2):
                    at = sender * lay.piece + lay.whole * lay.own * SUB + m * (SUB // 2)
                    first, second = rows[0][at : at + SUB], rows[1][at : at + SUB]
                    put(t, sender * lay.own + m, jnp.where(low, first, swap(second)))
                    put(t, sender * lay.own + m + 1, jnp.where(low, swap(first), second))
            at = lay.rows + lay.whole * SUB
            first, second = rows[0][at : at + SUB], rows[1][at : at + SUB]
            put_truth(t, jnp.where(low, first, swap(second)))


def tiles_to_rows(lay, get, put):
    for r in range(lay.blocks):
        for sender in range(lay.senders):
            for a in range(lay.whole):
                for m in range(lay.own):
                    at = sender * lay.piece + (a * lay.own + m) * SUB
                    put(r, at, get(r * lay.whole + a, sender * lay.own + m))
            if lay.half:
                t = lay.blocks * lay.whole + r // 2
                low = low_half()
                for m in range(0, lay.own, 2):
                    at = sender * lay.piece + lay.whole * lay.own * SUB + m * (SUB // 2)
                    first = get(t, sender * lay.own + m)
                    second = get(t, sender * lay.own + m + 1)
                    if r % 2 == 0:
                        put(r, at, jnp.where(low, first, swap(second)))
                    else:
                        put(r, at, jnp.where(low, swap(first), second))


def crps_tile(x, y, w):
    members = len(x)
    inv_total = None
    pulls = [None] * members
    for i in range(members):
        for j in range(i + 1, members):
            d = x[i] - x[j]
            inv = lax.rsqrt(d * d + kernel_eps)
            dk = d * inv
            inv_total = inv if inv_total is None else inv_total + inv
            pulls[i] = dk if pulls[i] is None else pulls[i] + dk
            pulls[j] = -dk if pulls[j] is None else pulls[j] - dk
    pair_total = kernel_eps * inv_total
    miss_total = None
    grads = []
    for i in range(members):
        d = x[i] - y
        t = d * d + kernel_eps
        inv = lax.rsqrt(t)
        k = t * inv
        miss_total = k if miss_total is None else miss_total + k
        pair_total = pair_total + d * pulls[i]
        grads.append(w * (d * inv - pulls[i] * (1.0 / (members - 1))))
    score = miss_total * (1.0 / members) - pair_total * (1.0 / (members * (members - 1)))
    return w * score, grads


def crps_loop(lay, x_ref, y_ref, w_ref, total_ref):
    def step(t, total):
        x = [x_ref[t, m] for m in range(lay.members)]
        part, grads = crps_tile(x, y_ref[t], w_ref[t])
        for m in range(lay.members):
            x_ref[t, m] = grads[m]
        return total + part

    total_ref[...] = lax.fori_loop(0, lay.tiles, step, total_ref[...])


CHUNK = 256
NT = (((1,), (1,)), ((), ()))


def fwd_kernel(lay, lat_ref, w_in_ref, b_in_ref, w_out_ref, perm_ref, b_out_ref, hi_ref, lo_ref, pre_ref, a_ref, bias_scr):
    @pl.when(pl.program_id(0) == 0)
    def _():
        spread = None
        for m in range(lay.own):
            p = perm_ref[m]
            a_ref[m] = jnp.dot(p, w_out_ref[...], preferred_element_type=f32).astype(bf16)
            spread = p.astype(f32) if spread is None else spread + p.astype(f32)
        bias = jnp.broadcast_to(b_out_ref[...], (lay.block, b_out_ref.shape[1]))
        bias_scr[...] = lax.dot_general(
            spread, bias, NT, precision=lax.Precision.HIGHEST, preferred_element_type=f32
        )

    tile = lat_ref.shape[1]
    lat = lat_ref[...].reshape(lay.own * tile, lat_ref.shape[2])
    field = None
    for c in range(0, w_in_ref.shape[1], CHUNK):
        cols = slice(c, c + CHUNK)
        pre = jnp.dot(lat, w_in_ref[:, cols], preferred_element_type=f32) + b_in_ref[:, cols]
        inner = pre * (GELU_C + (GELU_C * GELU_A) * (pre * pre))
        half = 0.5 * pre
        hidden = (half + half * jnp.tanh(inner)).astype(bf16)
        for m in range(lay.own):
            rows = slice(m * tile, (m + 1) * tile)
            pre_ref[m, :, cols] = pre[rows].astype(bf16)
            part = lax.dot_general(a_ref[m, :, cols], hidden[rows], NT, preferred_element_type=f32)
            field = part if field is None else field + part
    for r in range(hi_ref.shape[1]):
        block = field[:, r * lay.block : (r + 1) * lay.block] + bias_scr[...]
        for sender in range(lay.senders):
            part = block[sender * lay.piece : (sender + 1) * lay.piece]
            hi = part.astype(bf16)
            hi_ref[sender, r] = hi
            lo_ref[sender, r] = (part - hi.astype(f32)).astype(bf16)


SLAB = 16


def prep_kernel(lay, slots, vw_ref, count_ref, pre_ref, sm_ref, area_ref, slope_ref, wb_ref, w_ref):
    step = pl.program_id(0)
    rows = pre_ref.shape[1]

    @pl.when(step == 0)
    def _():
        kind = lax.broadcasted_iota(jnp.int32, (lay.truth_rows, lay.block), 0)
        column = jnp.zeros((lay.truth_rows, lay.block), f32)
        for v in range(lay.vars):
            column = jnp.where(kind == v, vw_ref[v], column)

        def weights(r):
            return column * area_ref[:, r * lay.block : (r + 1) * lay.block]

        for r in range(lay.blocks):
            w = weights(r)
            for a in range(lay.whole):
                w_ref[r * lay.whole + a] = w[a * SUB : (a + 1) * SUB]
            if lay.half and r % 2:
                at = lay.whole * SUB
                first, second = weights(r - 1)[at : at + SUB], w[at : at + SUB]
                w_ref[lay.blocks * lay.whole + r // 2] = jnp.where(low_half(), first, swap(second))

    for m in range(lay.own):

        def slab(i, carry):
            at = pl.ds(pl.multiple_of(i * SLAB, SLAB), SLAB)
            x = pre_ref[m, at, :].astype(f32)
            p = GELU_C + (GELU_C * GELU_A) * (x * x)
            up = 0.5 + 0.5 * jnp.tanh(x * p)
            bend = (x * (6.0 * p - 4.0 * GELU_C)) * (1.0 - up)
            slope_ref[m, at, :] = (up + up * bend).astype(bf16)
            return carry

        lax.fori_loop(0, rows // SLAB, slab, 0)

    for s in range(sm_ref.shape[0]):
        for k in range(slots):
            live = (k < count_ref[s, step]).astype(f32)
            wb_ref[s, 0, k * lay.block : (k + 1) * lay.block, :] = (sm_ref[s, 0, k] * live).astype(bf16)


def pack_kernel(lay, field_ref, target_ref, out_ref):
    for r in range(lay.blocks):
        field = field_ref[:, r].astype(f32).reshape(lay.rows, lay.block)
        truth = target_ref[:, r * lay.block : (r + 1) * lay.block]
        fill = jnp.zeros((lay.truth_rows - lay.vars, lay.block), f32)
        out_ref[r, : lay.rows] = field.astype(bf16)
        out_ref[r, lay.rows :] = jnp.concatenate([truth, fill], 0).astype(bf16)


def raw_kernel(lay, hi_ref, lo_ref, target_ref, w_ref, grad_ref, total_ref, x_scr, y_scr):
    def take(r):
        field = hi_ref[:, r].astype(f32) + lo_ref[:, r].astype(f32)
        truth = target_ref[:, r * lay.block : (r + 1) * lay.block]
        fill = jnp.zeros((lay.truth_rows - lay.vars, lay.block), f32)
        return jnp.concatenate([field.reshape(lay.rows, lay.block), truth, fill], 0)

    def put(t, m, tile):
        x_scr[t, m] = tile

    def put_truth(t, tile):
        y_scr[t] = tile

    rows_to_tiles(lay, take, put, put_truth)
    total_ref[...] = jnp.zeros_like(total_ref)
    crps_loop(lay, x_scr, y_scr, w_ref, total_ref)

    def put_rows(r, at, tile):
        grad_ref[r, at : at + SUB] = tile

    tiles_to_rows(lay, lambda t, m: x_scr[t, m], put_rows)


def scales_kernel(lay, slots, pos_ref, own_ref, inner_ref, outer_ref, wb_ref, w_ref, center_ref, to_inner_ref, to_outer_ref, total_ref, ext_scr, x_scr, y_scr, row_scr, adj_scr):
    scales = wb_ref.shape[0]
    block = lay.block
    n = lay.blocks
    for at, src in enumerate((own_ref, inner_ref, outer_ref)):
        ext_scr[at * n : (at + 1) * n] = src[...]
    total_ref[...] = jnp.zeros_like(total_ref)
    adj_scr[...] = jnp.zeros_like(adj_scr)
    for s in range(scales):

        def take(r):
            gathered = jnp.concatenate([ext_scr[pos_ref[s, r, k]] for k in range(slots)], 1)
            return jnp.dot(gathered, wb_ref[s, r], preferred_element_type=f32)

        def put(t, m, tile):
            x_scr[t, m] = tile

        def put_truth(t, tile):
            y_scr[t] = tile

        rows_to_tiles(lay, take, put, put_truth)
        crps_loop(lay, x_scr, y_scr, w_ref, total_ref)

        def put_rows(r, at, tile):
            row_scr[r, at : at + SUB] = tile

        tiles_to_rows(lay, lambda t, m: x_scr[t, m], put_rows)
        for r in range(n):
            back = lax.dot_general(row_scr[r].astype(bf16), wb_ref[s, r], NT, preferred_element_type=f32)
            for k in range(slots):
                p = pos_ref[s, r, k]
                adj_scr[p] = adj_scr[p] + back[:, k * block : (k + 1) * block]
    center_ref[...] = adj_scr[0:n]
    to_inner_ref[...] = adj_scr[n : 2 * n].astype(bf16)
    to_outer_ref[...] = adj_scr[2 * n : 3 * n].astype(bf16)


LOSS_ROWS = 16


def join_kernel(lay, center_ref, base_ref, a_ref, b_ref, ta_ref, tb_ref, out_ref):
    total = jnp.broadcast_to(jnp.sum(ta_ref[...] + tb_ref[...]), (LOSS_ROWS, lay.block))
    high = total.astype(bf16).astype(f32)
    mid = (total - high).astype(bf16).astype(f32)
    kind = lax.broadcasted_iota(jnp.int32, (LOSS_ROWS, lay.block), 0)
    tail = jnp.where(kind == 0, high, jnp.where(kind == 1, mid, jnp.where(kind == 2, total - high - mid, 0.0)))
    for sender in range(lay.senders):
        rows = slice(sender * lay.piece, (sender + 1) * lay.piece)
        parts = []
        for r in range(lay.blocks):
            local = center_ref[r, rows] + base_ref[r, rows]
            parts.append(local + (a_ref[r, rows].astype(f32) + b_ref[r, rows].astype(f32)))
        out_ref[sender] = jnp.concatenate(parts + [tail], 0).astype(bf16)


def bwd_kernel(lay, g_ref, a_ref, slope_ref, w_in_ref, out_ref):
    tile = out_ref.shape[1]
    count = tile // lay.block
    span = count * lay.piece
    at = pl.ds(pl.multiple_of(pl.program_id(0) * span, 16), span)
    g = g_ref[:, at, :].astype(f32)
    cols = []
    for r in range(count):
        rows = g[:, r * lay.piece : (r + 1) * lay.piece].reshape(lay.rows, lay.block)
        cols.append(rows.T.astype(bf16))
    grads = jnp.concatenate(cols, 0)
    parts = []
    for m in range(lay.own):
        hidden_grad = jnp.dot(grads, a_ref[m], preferred_element_type=f32)
        parts.append((hidden_grad * slope_ref[m].astype(f32)).astype(bf16))
    pre_grad = jnp.concatenate(parts, 0)
    for c in range(0, w_in_ref.shape[0], CHUNK):
        cols = slice(c, c + CHUNK)
        part = lax.dot_general(pre_grad, w_in_ref[cols, :], NT, preferred_element_type=f32).astype(bf16)
        for m in range(lay.own):
            out_ref[m, :, cols] = part[m * tile : (m + 1) * tile]


def params(mib):
    return pltpu.CompilerParams(vmem_limit_bytes=mib * 1024 * 1024)


def cost(flops, nbytes, trans=0):
    return pl.CostEstimate(flops=int(flops), bytes_accessed=int(nbytes), transcendentals=int(trans))


VM = pl.BlockSpec(memory_space=pltpu.VMEM)
SM = pl.BlockSpec(memory_space=pltpu.SMEM)


def whole_spec(shape):
    return pl.BlockSpec(shape, lambda i: (0,) * len(shape))


def exchange(block, axis):
    n = lax.axis_size(axis)
    out = []
    for first in (0, 1):
        route = []
        for i in range(first, n - 1, 2):
            route += [(i, i + 1), (i + 1, i)]
        out.append(lax.ppermute(block[first] if isinstance(block, tuple) else block, axis, route))
    return out


def on_device(
    latents,
    w_in,
    b_in,
    w_out,
    b_out,
    target,
    area_weight,
    var_weight,
    smoothers,
    block_index,
    block_count,
):
    own, points, width = latents.shape
    hidden_width = w_in.shape[1]
    var_total = w_out.shape[1]
    var_local = target.shape[0]
    scales, blocks, slots, block, _ = smoothers.shape
    senders = lax.axis_size("member")
    devices_grid = lax.axis_size("grid")
    lay = Layout(senders, own, var_local, blocks, block)
    perm = jnp.asarray(lay.permutation().transpose(0, 2, 1), bf16)
    payload = (senders, blocks, lay.piece, block)

    tile = min(points, 256)
    steps = points // tile
    tile_blocks = tile // block
    payload_spec = pl.BlockSpec((senders, tile_blocks, lay.piece, block), lambda i: (0, i, 0, 0))
    wide_spec = pl.BlockSpec((own, tile, hidden_width), lambda i: (0, i, 0))
    a_shape = (own, lay.rows, hidden_width)
    hi, lo, pre, spread_out = pl.pallas_call(
        functools.partial(fwd_kernel, lay),
        grid=(steps,),
        in_specs=[
            pl.BlockSpec((own, tile, width), lambda i: (0, i, 0)),
            whole_spec(w_in.shape),
            whole_spec((1, hidden_width)),
            whole_spec((var_total, hidden_width)),
            whole_spec(perm.shape),
            whole_spec((1, var_total)),
        ],
        out_specs=[payload_spec, payload_spec, wide_spec, whole_spec(a_shape)],
        out_shape=[
            jax.ShapeDtypeStruct(payload, bf16),
            jax.ShapeDtypeStruct(payload, bf16),
            jax.ShapeDtypeStruct((own, points, hidden_width), bf16),
            jax.ShapeDtypeStruct(a_shape, bf16),
        ],
        scratch_shapes=[pltpu.VMEM((lay.rows, lay.block), f32)],
        compiler_params=params(60),
        cost_estimate=cost(2 * own * points * width * hidden_width, 12e6, own * points * hidden_width),
        name="fwd",
    )(latents, w_in, b_in.reshape(1, -1), w_out.T, perm, b_out.reshape(1, -1))

    with jax.named_scope("hi"):
        own_hi = lax.all_to_all(hi, "member", split_axis=0, concat_axis=0, tiled=True)

    grad_shape = (blocks, lay.rows, block)
    tile_shape = (lay.tiles, lay.members, SUB, block)
    prep_tile = points // blocks
    with jax.named_scope("prep"):
        slope, wb, w_tiles = pl.pallas_call(
            functools.partial(prep_kernel, lay, slots),
            grid=(blocks,),
            in_specs=[
                SM,
                SM,
                pl.BlockSpec((own, prep_tile, hidden_width), lambda i: (0, i, 0)),
                pl.BlockSpec((scales, 1, slots, block, block), lambda i: (0, i, 0, 0, 0)),
                whole_spec((1, points)),
            ],
            out_specs=[
                pl.BlockSpec((own, prep_tile, hidden_width), lambda i: (0, i, 0)),
                pl.BlockSpec((scales, 1, slots * block, block), lambda i: (0, i, 0, 0)),
                whole_spec((lay.tiles, SUB, block)),
            ],
            out_shape=[
                jax.ShapeDtypeStruct((own, points, hidden_width), bf16),
                jax.ShapeDtypeStruct((scales, blocks, slots * block, block), bf16),
                jax.ShapeDtypeStruct((lay.tiles, SUB, block), f32),
            ],
            compiler_params=params(57),
            cost_estimate=cost(1e8, 1.4e7, own * points * hidden_width),
            name="prep",
        )(var_weight, block_count, pre, smoothers, area_weight.reshape(1, -1))
        rank = lax.axis_index("grid")
        offset = block_index - rank * blocks
        odd = rank % 2
        lower_part, upper_part = 2 - odd, 1 + odd
        part = jnp.where(offset < 0, lower_part, jnp.where(offset >= blocks, upper_part, 0))
        positions = jnp.clip(part * blocks + offset % blocks, 0, 3 * blocks - 1)
        _, own_hi = lax.optimization_barrier((wb, own_hi))

    with jax.named_scope("pack"):
        joint = pl.pallas_call(
            functools.partial(pack_kernel, lay),
            in_specs=[VM, VM],
            out_specs=VM,
            out_shape=jax.ShapeDtypeStruct((blocks, lay.total_rows, block), bf16),
            compiler_params=params(8),
            cost_estimate=cost(1e6, 1e6),
            name="pack",
        )(own_hi, target)
    with jax.named_scope("halo"):
        inner, outer = exchange(joint, "grid")
    _, lo = lax.optimization_barrier((joint, lo))
    with jax.named_scope("lo"):
        own_lo = lax.all_to_all(lo, "member", split_axis=0, concat_axis=0, tiled=True)

    center, to_inner, to_outer, total = pl.pallas_call(
        functools.partial(scales_kernel, lay, slots),
        in_specs=[SM] + [VM] * 5,
        out_specs=[VM] * 4,
        out_shape=[
            jax.ShapeDtypeStruct(grad_shape, f32),
            jax.ShapeDtypeStruct(grad_shape, bf16),
            jax.ShapeDtypeStruct(grad_shape, bf16),
            jax.ShapeDtypeStruct((SUB, block), f32),
        ],
        scratch_shapes=[
            pltpu.VMEM((3 * blocks, lay.total_rows, block), bf16),
            pltpu.VMEM(tile_shape, f32),
            pltpu.VMEM((lay.tiles, SUB, block), f32),
            pltpu.VMEM(grad_shape, f32),
            pltpu.VMEM((3 * blocks, lay.rows, block), f32),
        ],
        compiler_params=params(16),
        cost_estimate=cost(2e9, 8e6, 4e6),
        name="scales",
    )(positions, joint, inner, outer, wb, w_tiles)

    with jax.named_scope("rims"):
        from_inner, from_outer = exchange((to_inner, to_outer), "grid")
    with jax.named_scope("raw"):
        _, own_lo = lax.optimization_barrier((total, own_lo))
        base, total_raw = pl.pallas_call(
            functools.partial(raw_kernel, lay),
            in_specs=[VM] * 4,
            out_specs=[VM, VM],
            out_shape=[
                jax.ShapeDtypeStruct(grad_shape, f32),
                jax.ShapeDtypeStruct((SUB, block), f32),
            ],
            scratch_shapes=[pltpu.VMEM(tile_shape, f32), pltpu.VMEM((lay.tiles, SUB, block), f32)],
            compiler_params=params(8),
            cost_estimate=cost(5e8, 3e6, 2e6),
            name="raw",
        )(own_hi, own_lo, target, w_tiles)

    joined = pl.pallas_call(
        functools.partial(join_kernel, lay),
        in_specs=[VM] * 6,
        out_specs=VM,
        out_shape=jax.ShapeDtypeStruct((senders, blocks * lay.piece + LOSS_ROWS, block), bf16),
        compiler_params=params(8),
        cost_estimate=cost(1e6, 2e6),
        name="join",
    )(center, base, from_inner, from_outer, total, total_raw)
    with jax.named_scope("back"):
        field_grad = lax.all_to_all(joined, "member", split_axis=0, concat_axis=0, tiled=True)
    with jax.named_scope("loss"):
        head = blocks * lay.piece
        by_member = jnp.sum(field_grad[:, head : head + 3, :].astype(f32), (0, 1))
        by_member = jnp.broadcast_to(by_member[None, None, :], (devices_grid, 1, block))
        parts = lax.all_to_all(by_member, "grid", split_axis=0, concat_axis=0, tiled=True)
        loss = jnp.sum(parts[:, 0, 0]) / ((scales + 1) * var_total * points * devices_grid)

    grad = pl.pallas_call(
        functools.partial(bwd_kernel, lay),
        grid=(steps,),
        in_specs=[
            whole_spec(joined.shape),
            whole_spec(a_shape),
            wide_spec,
            whole_spec(w_in.shape),
        ],
        out_specs=pl.BlockSpec((own, tile, width), lambda i: (0, i, 0)),
        out_shape=jax.ShapeDtypeStruct((own, points, width), bf16),
        compiler_params=params(58),
        cost_estimate=cost(2 * own * points * width * hidden_width, 12e6),
        name="bwd",
    )(field_grad, spread_out, slope, w_in)
    return grad, loss


def solution(mesh):
    in_specs = (
        P("member", "grid", None),
        P(),
        P(),
        P(),
        P(),
        P("member", "grid"),
        P("grid"),
        P("member"),
        P(None, "grid", None, None, None),
        P(None, "grid", None),
        P(None, "grid"),
    )
    out_specs = (P("member", "grid", None), P())
    return jax.shard_map(
        on_device, mesh=mesh, in_specs=in_specs, out_specs=out_specs, check_vma=False
    )
```
